32 devices in a mesh: mode: 4 (over y, x), rest: 8 (over z, core).
Axes of the slice: x: 2, y: 2, z: 4, core: 2. Of those that a mesh axis runs over, the one named last changes fastest.
Arguments:
- unfolded: float32 [512, 65536], P('mode', 'rest'), may hold values from -150 to 150
- start_block: float32 [512, 128], replicated, may hold values from -6 to 6
Outputs:
- triangle: float32 [512, 512], replicated
- factor: float32 [512, 128], replicated
- core: float32 [128, 65536], P('mode', 'rest')
The draws below stay inside these ranges and needn't reach their ends.
All inputs are finite; a program needn't handle non-finite values.
Results may differ from the reference program's by a relative error of at most 0.0003.
Values sent between devices are 32-bit elements; how exact they have to be, the bound alone decides.
A program may use at most 64 MiB of HBM per device.

```python
import math
import jax
import jax.numpy as jnp
from jax import lax

M = 512
R = 128
ITERS = 3
COLS = 65536


def draw_unfolded(key, part):
    keys = jax.random.split(jax.random.fold_in(key, 11), 4)
    noise = jax.random.truncated_normal(keys[0], -5.0, 5.0, (M, COLS), jnp.float32)
    col_low = math.log(0.7)
    col_high = math.log(1.4)
    mixing = jnp.eye(M, dtype=jnp.float32) + 0.03 * jax.random.normal(keys[1], (M, M), jnp.float32)
    row_scale = jnp.exp(jax.random.uniform(keys[2], (M,), jnp.float32, 0.0, math.log(4.0)))
    position = jnp.arange(COLS, dtype=jnp.float32) / COLS
    col_scale = (1.0 + 2.0 * position) * jnp.exp(jax.random.uniform(keys[3], (COLS,), jnp.float32, col_low, col_high))
    mixed = jnp.dot(mixing, noise, precision=lax.Precision.HIGHEST)
    return row_scale[:, None] * mixed * col_scale[None, :]


def gaussian(stream_key, extent, width, reach, kind=jnp.bfloat16):
    values = width * jax.random.normal(stream_key, extent, jnp.float32)
    return jnp.clip(values, min=-reach, max=reach).astype(kind)


def setup_inputs(seed: int = 0) -> dict:
    key_list = jax.random.split(jax.random.key(seed), 3)
    unfolded = draw_unfolded(jax.random.fold_in(key_list[2], 71), 0)
    start_block = gaussian(key_list[1], (M, R), 1.0, 6.0, jnp.float32)
    return dict(unfolded=unfolded, start_block=start_block)


def orthogonal_steps(triangle, start_block):
    highest = lax.Precision.HIGHEST
    columns_now = start_block
    for repeat in range(ITERS):
        inner = jnp.dot(triangle.T, columns_now, precision=highest)
        image = jnp.dot(triangle, inner, precision=highest)
        projected = jnp.dot(image.T, image, precision=highest)
        small_factor = jnp.linalg.cholesky(projected)
        columns_now = lax.linalg.triangular_solve(small_factor, image, left_side=False, lower=True, transpose_a=True)
    return columns_now

def reference(unfolded, start_block):
    highest = lax.Precision.HIGHEST
    gram = jnp.dot(unfolded, unfolded.T, precision=highest) / COLS
    triangle = jnp.linalg.cholesky(gram)
    factor = orthogonal_steps(triangle, start_block)
    core = jnp.dot(factor.T, unfolded, precision=highest)
    return (triangle, factor, core)
```

```python
import functools

import jax
import jax.numpy as jnp
from jax import lax
from jax.experimental import pallas as pl
from jax.experimental.pallas import tpu as pltpu
from jax.sharding import PartitionSpec as P

ITERS = 3
SUB = 8
LANES = 128
F32 = jnp.float32
BF16 = jnp.bfloat16


def parts3(x):
    hi = x.astype(BF16).astype(F32)
    rest = x - hi
    mid = rest.astype(BF16).astype(F32)
    return hi, mid, rest - mid


def dot3(x, y, dims):
    xh = x.astype(BF16)
    xl = (x - xh.astype(F32)).astype(BF16)
    yh = y.astype(BF16)
    yl = (y - yh.astype(F32)).astype(BF16)
    dot = functools.partial(lax.dot_general, dimension_numbers=(dims, ((), ())), preferred_element_type=F32)
    return dot(xh, yh) + (dot(xh, yl) + dot(xl, yh))


def dotf(x, y, dims):
    return lax.dot_general(
        x, y, (dims, ((), ())), precision=lax.Precision.HIGHEST, preferred_element_type=F32
    )


def eliminate(ref, row, col, width, block):
    r0 = pl.multiple_of(block * SUB, SUB)
    v = ref[pl.ds(row + r0, SUB), pl.ds(col, width)]
    sub = lax.broadcasted_iota(jnp.int32, (SUB, 1), 0)
    d = pltpu.roll(v[:, :LANES], lax.rem(LANES - r0, LANES), 1)
    pivots = jnp.ones((SUB, 1), F32)
    for k in range(SUB):
        c = d[:, k : k + 1]
        p = c[k : k + 1, :]
        f = jnp.where(sub > k, c / p, 0.0)
        pivots = jnp.where(sub == k, p, pivots)
        if k < SUB - 1:
            d = d - f * d[k : k + 1, :]
            v = v - f * v[k : k + 1, :]
    s = lax.rsqrt(pivots)
    s = s * (1.5 - 0.5 * pivots * s * s)
    v = v * s
    ref[pl.ds(row + r0, SUB), pl.ds(col, width)] = v
    lane = lax.broadcasted_iota(jnp.int32, (SUB, LANES), 1)
    keep = lane >= r0 + SUB
    hi, mid, lo = parts3(v)
    lh, lm, ll = (jnp.where(keep, x[:, :LANES], 0.0) for x in (hi, mid, lo))
    left = jnp.concatenate([lh, lh, lm, lm, lh, ll], axis=0).astype(BF16)
    right = jnp.concatenate([hi, mid, hi, mid, lo, hi], axis=0).astype(BF16)
    upd = lax.dot_general(left, right, (((0,), (0,)), ((), ())), preferred_element_type=F32)
    ref[pl.ds(row, LANES), pl.ds(col, width)] -= upd


def solve_kernel(gram_ref, start_ref, tri_ref, factor_ref, basis_ref, work, aug):
    m = gram_ref.shape[0]
    r = start_ref.shape[1]
    rounds = m // LANES
    work[...] = gram_ref[...]

    def refill(basis_t):
        image_t = dotf(basis_t, gram_ref[...], ((1,), (0,)))
        aug[:, pl.ds(0, r)] = dotf(image_t, image_t, ((1,), (1,)))
        aug[:, pl.ds(r, m)] = image_t

    refill(start_ref[...].T)
    for t in range(max(rounds, ITERS)):
        base = t * LANES

        def step(block, carry):
            if t < rounds:
                eliminate(work, base, base, m - base, block)
            if t < ITERS:
                eliminate(aug, 0, 0, r + m, block)
            return carry

        lax.fori_loop(0, LANES // SUB, step, 0)
        if t < rounds - 1:
            tail = m - base - LANES
            u = work[pl.ds(base, LANES), pl.ds(base + LANES, tail)]
            work[pl.ds(base + LANES, tail), pl.ds(base + LANES, tail)] -= dotf(u, u, ((0,), (0,)))
        if t < ITERS - 1:
            refill(aug[:, pl.ds(r, m)])
    basis_t = aug[:, pl.ds(r, m)]
    basis_ref[...] = basis_t
    factor_ref[...] = basis_t.T
    upper = work[...]
    row = lax.broadcasted_iota(jnp.int32, (m, m), 0)
    colm = lax.broadcasted_iota(jnp.int32, (m, m), 1)
    tri_ref[...] = jnp.where(row <= colm, upper, 0.0).T


def solve(gram, start_block):
    m, r = start_block.shape
    vmem = pl.BlockSpec(memory_space=pltpu.VMEM)
    return pl.pallas_call(
        solve_kernel,
        out_shape=(
            jax.ShapeDtypeStruct((m, m), F32),
            jax.ShapeDtypeStruct((m, r), F32),
            jax.ShapeDtypeStruct((r, m), F32),
        ),
        in_specs=[vmem, vmem],
        out_specs=(vmem, vmem, vmem),
        scratch_shapes=[pltpu.VMEM((m, m), F32), pltpu.VMEM((r, r + m), F32)],
        compiler_params=pltpu.CompilerParams(vmem_limit_bytes=32 * 1024 * 1024),
        name="solve",
    )(gram, start_block)


def per_device(unfolded, start_block):
    high = lax.Precision.HIGH
    rows_dev, cols_dev = unfolded.shape
    total_cols = cols_dev * lax.axis_size("rest")
    full_rows = lax.all_to_all(unfolded, "mode", split_axis=1, concat_axis=0, tiled=True)
    gram_part = jnp.dot(full_rows, full_rows.T, precision=high) / total_cols
    gram = lax.psum(gram_part, ("mode", "rest"))
    triangle, factor, basis_t = solve(gram, start_block)
    partial_value = jnp.dot(basis_t, full_rows, precision=high)
    core = lax.all_to_all(partial_value, "mode", split_axis=0, concat_axis=1, tiled=True)
    return (triangle, factor, core)


def solution(mesh):
    return jax.shard_map(
        per_device,
        mesh=mesh,
        in_specs=(P("mode", "rest"), P()),
        out_specs=(P(), P(), P("mode", "rest")),
        check_vma=False,
    )
```

```python
import functools

import jax
import jax.numpy as jnp
from jax import lax
from jax.experimental import pallas as pl
from jax.experimental.pallas import tpu as pltpu
from jax.sharding import PartitionSpec as P

ITERS = 3
SUB = 8
LANES = 128
F32 = jnp.float32
BF16 = jnp.bfloat16
MESH = pl.DeviceIdType.MESH


def parts3(x):
    hi = x.astype(BF16).astype(F32)
    rest = x - hi
    mid = rest.astype(BF16).astype(F32)
    return hi, mid, rest - mid


def dot3(x, y, dims):
    xh = x.astype(BF16)
    xl = (x - xh.astype(F32)).astype(BF16)
    yh = y.astype(BF16)
    yl = (y - yh.astype(F32)).astype(BF16)
    dot = functools.partial(lax.dot_general, dimension_numbers=(dims, ((), ())), preferred_element_type=F32)
    return dot(xh, yh) + (dot(xh, yl) + dot(xl, yh))


def dotf(x, y, dims):
    return lax.dot_general(
        x, y, (dims, ((), ())), precision=lax.Precision.HIGHEST, preferred_element_type=F32
    )


def eliminate(ref, row, col, width, block):
    r0 = pl.multiple_of(block * SUB, SUB)
    v = ref[pl.ds(row + r0, SUB), pl.ds(col, width)]
    sub = lax.broadcasted_iota(jnp.int32, (SUB, 1), 0)
    d = pltpu.roll(v[:, :LANES], lax.rem(LANES - r0, LANES), 1)
    pivots = jnp.ones((SUB, 1), F32)
    for k in range(SUB):
        c = d[:, k : k + 1]
        p = c[k : k + 1, :]
        f = jnp.where(sub > k, c / p, 0.0)
        pivots = jnp.where(sub == k, p, pivots)
        if k < SUB - 1:
            d = d - f * d[k : k + 1, :]
            v = v - f * v[k : k + 1, :]
    s = lax.rsqrt(pivots)
    s = s * (1.5 - 0.5 * pivots * s * s)
    v = v * s
    ref[pl.ds(row + r0, SUB), pl.ds(col, width)] = v
    lane = lax.broadcasted_iota(jnp.int32, (SUB, LANES), 1)
    keep = lane >= r0 + SUB
    hi, mid, lo = parts3(v)
    lh, lm, ll = (jnp.where(keep, x[:, :LANES], 0.0) for x in (hi, mid, lo))
    left = jnp.concatenate([lh, lh, lm, lm, lh, ll], axis=0).astype(BF16)
    right = jnp.concatenate([hi, mid, hi, mid, lo, hi], axis=0).astype(BF16)
    upd = lax.dot_general(left, right, (((0,), (0,)), ((), ())), preferred_element_type=F32)
    ref[pl.ds(row, LANES), pl.ds(col, width)] -= upd


def block_pairs(count):
    return [(i, j) for i in range(count) for j in range(i, count)]


def solve_kernel(packed_ref, start_ref, tri_ref, factor_ref, basis_ref, gram_ref, work, aug):
    m, r = start_ref.shape
    rounds = m // LANES
    for at, (i, j) in enumerate(block_pairs(rounds)):
        piece = packed_ref[pl.ds(at * LANES, LANES), :]
        spot = (pl.ds(i * LANES, LANES), pl.ds(j * LANES, LANES))
        gram_ref[spot] = piece
        work[spot] = piece
        if i != j:
            gram_ref[spot[::-1]] = piece.T

    def refill(basis_t):
        image_t = dotf(basis_t, gram_ref[...], ((1,), (0,)))
        aug[:, pl.ds(0, r)] = dotf(image_t, image_t, ((1,), (1,)))
        aug[:, pl.ds(r, m)] = image_t

    refill(start_ref[...].T)
    for t in range(max(rounds, ITERS)):
        base = t * LANES

        def step(block, carry):
            if t < rounds:
                eliminate(work, base, base, m - base, block)
            if t < ITERS:
                eliminate(aug, 0, 0, r + m, block)
            return carry

        lax.fori_loop(0, LANES // SUB, step, 0)
        if t < rounds - 1:
            tail = m - base - LANES
            u = work[pl.ds(base, LANES), pl.ds(base + LANES, tail)]
            work[pl.ds(base + LANES, tail), pl.ds(base + LANES, tail)] -= dotf(u, u, ((0,), (0,)))
        if t < ITERS - 1:
            refill(aug[:, pl.ds(r, m)])
    basis_t = aug[:, pl.ds(r, m)]
    basis_ref[...] = basis_t
    factor_ref[...] = basis_t.T
    row = lax.broadcasted_iota(jnp.int32, (LANES, LANES), 0)
    col = lax.broadcasted_iota(jnp.int32, (LANES, LANES), 1)
    for i in range(rounds):
        for j in range(rounds):
            spot = (pl.ds(j * LANES, LANES), pl.ds(i * LANES, LANES))
            if j < i:
                tri_ref[spot] = jnp.zeros((LANES, LANES), F32)
                continue
            piece = work[spot[::-1]]
            tri_ref[spot] = (jnp.where(row <= col, piece, 0.0) if i == j else piece).T


def solve(packed, start_block):
    m, r = start_block.shape
    vmem = pl.BlockSpec(memory_space=pltpu.VMEM)
    return pl.pallas_call(
        solve_kernel,
        out_shape=(
            jax.ShapeDtypeStruct((m, m), F32),
            jax.ShapeDtypeStruct((m, r), F32),
            jax.ShapeDtypeStruct((r, m), F32),
        ),
        in_specs=[vmem, vmem],
        out_specs=(vmem, vmem, vmem),
        scratch_shapes=[pltpu.VMEM((m, m), F32), pltpu.VMEM((m, m), F32), pltpu.VMEM((r, r + m), F32)],
        compiler_params=pltpu.CompilerParams(vmem_limit_bytes=32 * 1024 * 1024),
        name="solve",
    )(packed, start_block)


def sum_kernel(shape, in_ref, out_ref, got1, got2, got3, sum1, sum2, send, recv):
    modes, cores, depth = shape
    me_mode = lax.axis_index("mode")
    me_rest = lax.axis_index("rest")
    me_core = lax.rem(me_rest, cores)
    me_z = me_rest // cores
    mine = (me_core, me_mode, me_z)
    sizes = (cores, modes, depth)
    rows = [in_ref.shape[0] // cores]
    rows.append(rows[0] // modes)
    rows.append(rows[1] // depth)

    def peer(stage, off):
        other = lax.rem(mine[stage] + off, sizes[stage])
        spot = [me_core, me_mode, me_z]
        spot[stage] = other
        return other, (spot[1], spot[2] * cores + spot[0])

    barrier = pltpu.get_barrier_semaphore()
    for stage in range(3):
        def greet(off, carry):
            _, device = peer(stage, off)
            pl.semaphore_signal(barrier, inc=1, device_id=device, device_id_type=MESH)
            return carry
        lax.fori_loop(1, sizes[stage], greet, 0)
    pl.semaphore_wait(barrier, sum(sizes) - 3)

    def at(start, size):
        return pl.ds(pl.multiple_of(start, SUB), size)

    def exchange(phase, stage, source, target):
        def copy(off):
            other, device = peer(stage, off)
            return pltpu.make_async_remote_copy(
                src_ref=source(other),
                dst_ref=target(mine[stage], off),
                send_sem=send.at[phase, off],
                recv_sem=recv.at[phase, off],
                device_id=device,
                device_id_type=MESH,
            )
        def begin(off, carry):
            copy(off).start()
            return carry
        def end(off, carry):
            copy(off).wait()
            return carry
        lax.fori_loop(1, sizes[stage], begin, 0)
        lax.fori_loop(1, sizes[stage], end, 0)

    def total(stage, source, got):
        def add(off, value):
            return value + got[off - 1]
        return lax.fori_loop(1, sizes[stage], add, source[at(mine[stage] * rows[stage], rows[stage]), :])

    exchange(0, 0, lambda o: in_ref.at[at(o * rows[0], rows[0])], lambda o, off: got1.at[off - 1])
    sum1[...] = total(0, in_ref, got1)
    exchange(1, 1, lambda o: sum1.at[at(o * rows[1], rows[1])], lambda o, off: got2.at[off - 1])
    sum2[...] = total(1, sum1, got2)
    exchange(2, 2, lambda o: sum2.at[at(o * rows[2], rows[2])], lambda o, off: got3.at[off - 1])
    start2 = me_core * rows[0] + me_mode * rows[1]
    start3 = start2 + me_z * rows[2]
    out_ref[at(start3, rows[2]), :] = total(2, sum2, got3)
    for phase, stage, start, size in ((3, 2, start3, rows[2]), (4, 1, start2, rows[1]), (5, 0, me_core * rows[0], rows[0])):
        block = out_ref.at[at(start, size)]
        exchange(phase, stage, lambda o: block, lambda o, off: block)


def sum_all(packed, modes, rest):
    cores = 2 if rest % 2 == 0 else 1
    depth = rest // cores
    count = packed.shape[0]
    each = pl.cdiv(count, modes * rest * SUB) * SUB
    padded = each * modes * rest
    if padded != count:
        packed = jnp.pad(packed, ((0, padded - count), (0, 0)))
    width = packed.shape[1]
    vmem = pl.BlockSpec(memory_space=pltpu.VMEM)
    most = max(cores, modes, depth)
    return pl.pallas_call(
        functools.partial(sum_kernel, (modes, cores, depth)),
        out_shape=jax.ShapeDtypeStruct((padded, width), F32),
        in_specs=[vmem],
        out_specs=vmem,
        scratch_shapes=[
            pltpu.VMEM((max(cores - 1, 1), padded // cores, width), F32),
            pltpu.VMEM((max(modes - 1, 1), padded // (cores * modes), width), F32),
            pltpu.VMEM((max(depth - 1, 1), each, width), F32),
            pltpu.VMEM((padded // cores, width), F32),
            pltpu.VMEM((padded // (cores * modes), width), F32),
            pltpu.SemaphoreType.DMA((6, most)),
            pltpu.SemaphoreType.DMA((6, most)),
        ],
        compiler_params=pltpu.CompilerParams(collective_id=0, has_side_effects=True),
        name="sum_all",
    )(packed)[:count]


def per_device(unfolded, start_block):
    high = lax.Precision.HIGH
    rows_dev, cols_dev = unfolded.shape
    total_cols = cols_dev * lax.axis_size("rest")
    full_rows = lax.all_to_all(unfolded, "mode", split_axis=1, concat_axis=0, tiled=True)
    blocks = full_rows.shape[0] // LANES
    pieces = []
    for i in range(blocks):
        strip = jnp.dot(full_rows[i * LANES : (i + 1) * LANES], full_rows[i * LANES :].T, precision=high) / total_cols
        pieces += [strip[:, j * LANES : (j + 1) * LANES] for j in range(blocks - i)]
    packed = jnp.concatenate(pieces, axis=0)
    packed = sum_all(packed, lax.axis_size("mode"), lax.axis_size("rest"))
    triangle, factor, basis_t = solve(packed, start_block)
    partial_value = jnp.dot(basis_t, full_rows, precision=high)
    core = lax.all_to_all(partial_value, "mode", split_axis=0, concat_axis=1, tiled=True)
    return (triangle, factor, core)


def solution(mesh):
    return jax.shard_map(
        per_device,
        mesh=mesh,
        in_specs=(P("mode", "rest"), P()),
        out_specs=(P(), P(), P("mode", "rest")),
        check_vma=False,
    )
```

```python
import functools

import jax
import jax.numpy as jnp
from jax import lax
from jax.experimental import pallas as pl
from jax.experimental.pallas import tpu as pltpu
from jax.sharding import PartitionSpec as P

ITERS = 3
SUB = 8
STEP = 16
LANES = 128
F32 = jnp.float32
BF16 = jnp.bfloat16
MESH = pl.DeviceIdType.MESH


def parts3(x):
    hi = x.astype(BF16).astype(F32)
    rest = x - hi
    mid = rest.astype(BF16).astype(F32)
    return hi, mid, rest - mid


def dot3(x, y, dims):
    xh = x.astype(BF16)
    xl = (x - xh.astype(F32)).astype(BF16)
    yh = y.astype(BF16)
    yl = (y - yh.astype(F32)).astype(BF16)
    dot = functools.partial(lax.dot_general, dimension_numbers=(dims, ((), ())), preferred_element_type=F32)
    return dot(xh, yh) + (dot(xh, yl) + dot(xl, yh))


def dotf(x, y, dims):
    return lax.dot_general(
        x, y, (dims, ((), ())), precision=lax.Precision.HIGHEST, preferred_element_type=F32
    )


def eliminate(ref, row, col, width, block):
    r0 = pl.multiple_of(block * STEP, STEP)
    chunks = [ref[pl.ds(row + r0, STEP), pl.ds(col + c, LANES)] for c in range(0, width, LANES)]
    sub = lax.broadcasted_iota(jnp.int32, (STEP, LANES), 0)
    cols = [
        jnp.take_along_axis(chunks[0], jnp.full((STEP, LANES), r0 + k, jnp.int32), axis=1) for k in range(STEP)
    ]
    pivots = jnp.ones((STEP, LANES), F32)
    for k in range(STEP):
        p = cols[k][k : k + 1, :]
        f = jnp.where(sub > k, cols[k] * (1.0 / p), 0.0)
        pivots = jnp.where(sub == k, p, pivots)
        for j in range(k + 1, STEP):
            cols[j] = cols[j] - f * cols[j][k : k + 1, :]
        chunks = [v - f * v[k : k + 1, :] for v in chunks]
    s = lax.rsqrt(pivots)
    s = s * (1.5 - 0.5 * pivots * s * s)
    chunks = [v * s for v in chunks]
    v = jnp.concatenate(chunks, axis=1)
    ref[pl.ds(row + r0, STEP), pl.ds(col, width)] = v
    lane = lax.broadcasted_iota(jnp.int32, (STEP, LANES), 1)
    keep = lane >= r0 + STEP
    hi, mid, lo = parts3(v)
    lh, lm, ll = (jnp.where(keep, x[:, :LANES], 0.0) for x in (hi, mid, lo))
    left = jnp.concatenate([lh, lh, lm, lm, lh, ll], axis=0).astype(BF16)
    right = jnp.concatenate([hi, mid, hi, mid, lo, hi], axis=0).astype(BF16)
    upd = lax.dot_general(left, right, (((0,), (0,)), ((), ())), preferred_element_type=F32)
    ref[pl.ds(row, LANES), pl.ds(col, width)] -= upd


def block_pairs(count):
    return [(i, j) for i in range(count) for j in range(i, count)]


def solve_kernel(packed_ref, start_ref, tri_ref, factor_ref, basis_ref, gram_ref, work, aug):
    m, r = start_ref.shape
    rounds = m // LANES
    for at, (i, j) in enumerate(block_pairs(rounds)):
        piece = packed_ref[pl.ds(at * LANES, LANES), :]
        spot = (pl.ds(i * LANES, LANES), pl.ds(j * LANES, LANES))
        gram_ref[spot] = piece
        work[spot] = piece
        if i != j:
            gram_ref[spot[::-1]] = piece.T

    def refill(basis_t):
        image_t = dotf(basis_t, gram_ref[...], ((1,), (0,)))
        aug[:, pl.ds(0, r)] = dotf(image_t, image_t, ((1,), (1,)))
        aug[:, pl.ds(r, m)] = image_t

    refill(start_ref[...].T)
    for t in range(max(rounds, ITERS)):
        base = t * LANES

        def step(block, carry):
            if t < rounds:
                eliminate(work, base, base, m - base, block)
            if t < ITERS:
                eliminate(aug, 0, 0, r + m, block)
            return carry

        lax.fori_loop(0, LANES // STEP, step, 0)
        if t < rounds - 1:
            tail = m - base - LANES
            u = work[pl.ds(base, LANES), pl.ds(base + LANES, tail)]
            work[pl.ds(base + LANES, tail), pl.ds(base + LANES, tail)] -= dotf(u, u, ((0,), (0,)))
        if t < ITERS - 1:
            refill(aug[:, pl.ds(r, m)])
    basis_t = aug[:, pl.ds(r, m)]
    basis_ref[...] = basis_t
    factor_ref[...] = basis_t.T
    row = lax.broadcasted_iota(jnp.int32, (LANES, LANES), 0)
    col = lax.broadcasted_iota(jnp.int32, (LANES, LANES), 1)
    for i in range(rounds):
        for j in range(rounds):
            spot = (pl.ds(j * LANES, LANES), pl.ds(i * LANES, LANES))
            if j < i:
                tri_ref[spot] = jnp.zeros((LANES, LANES), F32)
                continue
            piece = work[spot[::-1]]
            tri_ref[spot] = (jnp.where(row <= col, piece, 0.0) if i == j else piece).T


def solve(packed, start_block):
    m, r = start_block.shape
    vmem = pl.BlockSpec(memory_space=pltpu.VMEM)
    return pl.pallas_call(
        solve_kernel,
        out_shape=(
            jax.ShapeDtypeStruct((m, m), F32),
            jax.ShapeDtypeStruct((m, r), F32),
            jax.ShapeDtypeStruct((r, m), F32),
        ),
        in_specs=[vmem, vmem],
        out_specs=(vmem, vmem, vmem),
        scratch_shapes=[pltpu.VMEM((m, m), F32), pltpu.VMEM((m, m), F32), pltpu.VMEM((r, r + m), F32)],
        compiler_params=pltpu.CompilerParams(vmem_limit_bytes=32 * 1024 * 1024),
        name="solve",
    )(packed, start_block)


def sum_kernel(shape, in_ref, out_ref, got1, got2, got3, sum1, sum2, send, recv):
    modes, cores, depth = shape
    me_mode = lax.axis_index("mode")
    me_rest = lax.axis_index("rest")
    me_core = lax.rem(me_rest, cores)
    me_z = me_rest // cores
    mine = (me_core, me_mode, me_z)
    sizes = (cores, modes, depth)
    rows = [in_ref.shape[0] // cores]
    rows.append(rows[0] // modes)
    rows.append(rows[1] // depth)

    def peer(stage, off):
        other = lax.rem(mine[stage] + off, sizes[stage])
        spot = [me_core, me_mode, me_z]
        spot[stage] = other
        return other, (spot[1], spot[2] * cores + spot[0])

    barrier = pltpu.get_barrier_semaphore()
    for stage in range(3):
        def greet(off, carry):
            _, device = peer(stage, off)
            pl.semaphore_signal(barrier, inc=1, device_id=device, device_id_type=MESH)
            return carry
        lax.fori_loop(1, sizes[stage], greet, 0)
    pl.semaphore_wait(barrier, sum(sizes) - 3)

    def at(start, size):
        return pl.ds(pl.multiple_of(start, SUB), size)

    def exchange(phase, stage, source, target):
        def copy(off):
            other, device = peer(stage, off)
            return pltpu.make_async_remote_copy(
                src_ref=source(other),
                dst_ref=target(mine[stage], off),
                send_sem=send.at[phase, off],
                recv_sem=recv.at[phase, off],
                device_id=device,
                device_id_type=MESH,
            )
        def begin(off, carry):
            copy(off).start()
            return carry
        def end(off, carry):
            copy(off).wait()
            return carry
        lax.fori_loop(1, sizes[stage], begin, 0)
        lax.fori_loop(1, sizes[stage], end, 0)

    def total(stage, source, got):
        def add(off, value):
            return value + got[off - 1]
        return lax.fori_loop(1, sizes[stage], add, source[at(mine[stage] * rows[stage], rows[stage]), :])

    exchange(0, 0, lambda o: in_ref.at[at(o * rows[0], rows[0])], lambda o, off: got1.at[off - 1])
    sum1[...] = total(0, in_ref, got1)
    exchange(1, 1, lambda o: sum1.at[at(o * rows[1], rows[1])], lambda o, off: got2.at[off - 1])
    sum2[...] = total(1, sum1, got2)
    exchange(2, 2, lambda o: sum2.at[at(o * rows[2], rows[2])], lambda o, off: got3.at[off - 1])
    start2 = me_core * rows[0] + me_mode * rows[1]
    start3 = start2 + me_z * rows[2]
    out_ref[at(start3, rows[2]), :] = total(2, sum2, got3)
    for phase, stage, start, size in ((3, 2, start3, rows[2]), (4, 1, start2, rows[1]), (5, 0, me_core * rows[0], rows[0])):
        block = out_ref.at[at(start, size)]
        exchange(phase, stage, lambda o: block, lambda o, off: block)


def sum_all(packed, modes, rest):
    cores = 2 if rest % 2 == 0 else 1
    depth = rest // cores
    count = packed.shape[0]
    each = pl.cdiv(count, modes * rest * SUB) * SUB
    padded = each * modes * rest
    if padded != count:
        packed = jnp.pad(packed, ((0, padded - count), (0, 0)))
    width = packed.shape[1]
    vmem = pl.BlockSpec(memory_space=pltpu.VMEM)
    most = max(cores, modes, depth)
    return pl.pallas_call(
        functools.partial(sum_kernel, (modes, cores, depth)),
        out_shape=jax.ShapeDtypeStruct((padded, width), F32),
        in_specs=[vmem],
        out_specs=vmem,
        scratch_shapes=[
            pltpu.VMEM((max(cores - 1, 1), padded // cores, width), F32),
            pltpu.VMEM((max(modes - 1, 1), padded // (cores * modes), width), F32),
            pltpu.VMEM((max(depth - 1, 1), each, width), F32),
            pltpu.VMEM((padded // cores, width), F32),
            pltpu.VMEM((padded // (cores * modes), width), F32),
            pltpu.SemaphoreType.DMA((6, most)),
            pltpu.SemaphoreType.DMA((6, most)),
        ],
        compiler_params=pltpu.CompilerParams(collective_id=0, has_side_effects=True),
        name="sum_all",
    )(packed)[:count]


def per_device(unfolded, start_block):
    high = lax.Precision.HIGH
    rows_dev, cols_dev = unfolded.shape
    total_cols = cols_dev * lax.axis_size("rest")
    full_rows = lax.all_to_all(unfolded, "mode", split_axis=1, concat_axis=0, tiled=True)
    blocks = full_rows.shape[0] // LANES
    pieces = []
    for i in range(blocks):
        strip = jnp.dot(full_rows[i * LANES : (i + 1) * LANES], full_rows[i * LANES :].T, precision=high) / total_cols
        pieces += [strip[:, j * LANES : (j + 1) * LANES] for j in range(blocks - i)]
    packed = jnp.concatenate(pieces, axis=0)
    packed = sum_all(packed, lax.axis_size("mode"), lax.axis_size("rest"))
    triangle, factor, basis_t = solve(packed, start_block)
    partial_value = jnp.dot(basis_t, full_rows, precision=high)
    core = lax.all_to_all(partial_value, "mode", split_axis=0, concat_axis=1, tiled=True)
    return (triangle, factor, core)


def solution(mesh):
    return jax.shard_map(
        per_device,
        mesh=mesh,
        in_specs=(P("mode", "rest"), P()),
        out_specs=(P(), P(), P("mode", "rest")),
        check_vma=False,
    )
```

```python
import functools

import jax
import jax.numpy as jnp
from jax import lax
from jax.experimental import pallas as pl
from jax.experimental.pallas import tpu as pltpu
from jax.sharding import PartitionSpec as P

ITERS = 3
SUB = 8
STEP = 16
CHUNKS = 4
LANES = 128
F32 = jnp.float32
BF16 = jnp.bfloat16
MESH = pl.DeviceIdType.MESH


def parts3(x):
    hi = x.astype(BF16).astype(F32)
    rest = x - hi
    mid = rest.astype(BF16).astype(F32)
    return hi, mid, rest - mid


def nt(x, y):
    return lax.dot_general(x, y, (((1,), (1,)), ((), ())), preferred_element_type=F32)


def dotf(x, y, dims):
    return lax.dot_general(
        x, y, (dims, ((), ())), precision=lax.Precision.HIGHEST, preferred_element_type=F32
    )


def eliminate(ref, row, col, width, block):
    r0 = pl.multiple_of(block * STEP, STEP)
    chunks = [ref[pl.ds(row + r0, STEP), pl.ds(col + c, LANES)] for c in range(0, width, LANES)]
    sub = lax.broadcasted_iota(jnp.int32, (STEP, LANES), 0)
    cols = [
        jnp.take_along_axis(chunks[0], jnp.full((STEP, LANES), r0 + k, jnp.int32), axis=1) for k in range(STEP)
    ]
    pivots = jnp.ones((STEP, LANES), F32)
    for k in range(STEP):
        p = cols[k][k : k + 1, :]
        f = jnp.where(sub > k, cols[k] * (1.0 / p), 0.0)
        pivots = jnp.where(sub == k, p, pivots)
        for j in range(k + 1, STEP):
            cols[j] = cols[j] - f * cols[j][k : k + 1, :]
        chunks = [v - f * v[k : k + 1, :] for v in chunks]
    s = lax.rsqrt(pivots)
    s = s * (1.5 - 0.5 * pivots * s * s)
    chunks = [v * s for v in chunks]
    v = jnp.concatenate(chunks, axis=1)
    ref[pl.ds(row + r0, STEP), pl.ds(col, width)] = v
    lane = lax.broadcasted_iota(jnp.int32, (STEP, LANES), 1)
    keep = lane >= r0 + STEP
    hi, mid, lo = parts3(v)
    lh, lm, ll = (jnp.where(keep, x[:, :LANES], 0.0) for x in (hi, mid, lo))
    left = jnp.concatenate([lh, lh, lm, lm, lh, ll], axis=0).astype(BF16)
    right = jnp.concatenate([hi, mid, hi, mid, lo, hi], axis=0).astype(BF16)
    upd = lax.dot_general(left, right, (((0,), (0,)), ((), ())), preferred_element_type=F32)
    ref[pl.ds(row, LANES), pl.ds(col, width)] -= upd


def block_pairs(count):
    return [(i, j) for i in range(count) for j in range(i, count)]


def solve_kernel(packed_ref, start_ref, tri_ref, factor_ref, basis_ref, gram_ref, work, aug):
    m, r = start_ref.shape
    rounds = m // LANES
    for at, (i, j) in enumerate(block_pairs(rounds)):
        piece = packed_ref[pl.ds(at * LANES, LANES), :]
        spot = (pl.ds(i * LANES, LANES), pl.ds(j * LANES, LANES))
        gram_ref[spot] = piece
        work[spot] = piece
        if i != j:
            gram_ref[spot[::-1]] = piece.T

    def refill(basis_t):
        image_t = dotf(basis_t, gram_ref[...], ((1,), (0,)))
        aug[:, pl.ds(0, r)] = dotf(image_t, image_t, ((1,), (1,)))
        aug[:, pl.ds(r, m)] = image_t

    refill(start_ref[...].T)
    for t in range(max(rounds, ITERS)):
        base = t * LANES

        def step(block, carry):
            if t < rounds:
                eliminate(work, base, base, m - base, block)
            if t < ITERS:
                eliminate(aug, 0, 0, r + m, block)
            return carry

        lax.fori_loop(0, LANES // STEP, step, 0)
        if t < rounds - 1:
            tail = m - base - LANES
            u = work[pl.ds(base, LANES), pl.ds(base + LANES, tail)]
            work[pl.ds(base + LANES, tail), pl.ds(base + LANES, tail)] -= dotf(u, u, ((0,), (0,)))
        if t < ITERS - 1:
            refill(aug[:, pl.ds(r, m)])
    basis_t = aug[:, pl.ds(r, m)]
    basis_ref[...] = basis_t
    factor_ref[...] = basis_t.T
    row = lax.broadcasted_iota(jnp.int32, (LANES, LANES), 0)
    col = lax.broadcasted_iota(jnp.int32, (LANES, LANES), 1)
    for i in range(rounds):
        for j in range(rounds):
            spot = (pl.ds(j * LANES, LANES), pl.ds(i * LANES, LANES))
            if j < i:
                tri_ref[spot] = jnp.zeros((LANES, LANES), F32)
                continue
            piece = work[spot[::-1]]
            tri_ref[spot] = (jnp.where(row <= col, piece, 0.0) if i == j else piece).T


def solve(packed, start_block):
    m, r = start_block.shape
    vmem = pl.BlockSpec(memory_space=pltpu.VMEM)
    return pl.pallas_call(
        solve_kernel,
        out_shape=(
            jax.ShapeDtypeStruct((m, m), F32),
            jax.ShapeDtypeStruct((m, r), F32),
            jax.ShapeDtypeStruct((r, m), F32),
        ),
        in_specs=[vmem, vmem],
        out_specs=(vmem, vmem, vmem),
        scratch_shapes=[pltpu.VMEM((m, m), F32), pltpu.VMEM((m, m), F32), pltpu.VMEM((r, r + m), F32)],
        compiler_params=pltpu.CompilerParams(vmem_limit_bytes=32 * 1024 * 1024),
        name="solve",
    )(packed, start_block)


def gram_kernel(shape, total_cols, x_ref, full_out, out_ref, full, in_ref, got1, got2, got3, sum1, sum2,
                send, recv, row_send, row_recv, row_local, row_out):
    modes, cores, depth = shape
    me_mode = lax.axis_index("mode")
    me_rest = lax.axis_index("rest")
    me_core = lax.rem(me_rest, cores)
    me_z = me_rest // cores
    mine = (me_core, me_mode, me_z)
    sizes = (cores, modes, depth)
    rows = [in_ref.shape[0] // cores]
    rows.append(rows[0] // modes)
    rows.append(rows[1] // depth)

    def peer(stage, off):
        other = lax.rem(mine[stage] + off, sizes[stage])
        spot = [me_core, me_mode, me_z]
        spot[stage] = other
        return other, (spot[1], spot[2] * cores + spot[0])

    barrier = pltpu.get_barrier_semaphore()
    for stage in range(3):
        def greet(off, carry):
            _, device = peer(stage, off)
            pl.semaphore_signal(barrier, inc=1, device_id=device, device_id_type=MESH)
            return carry
        lax.fori_loop(1, sizes[stage], greet, 0)
    pl.semaphore_wait(barrier, sum(sizes) - 3)

    rows_dev = x_ref.shape[0]
    m, width = full.shape
    chunk = width // CHUNKS
    copies = []
    for c in range(CHUNKS):
        batch = []
        spot = (pl.ds(pl.multiple_of(me_mode * rows_dev, rows_dev), rows_dev), pl.ds(c * chunk, chunk))
        for off in range(1, modes):
            other, device = peer(1, off)
            batch.append(pltpu.make_async_remote_copy(
                src_ref=x_ref.at[:, pl.ds(pl.multiple_of(other * width + c * chunk, chunk), chunk)],
                dst_ref=full.at[spot],
                send_sem=row_send.at[c, off],
                recv_sem=row_recv.at[c, off],
                device_id=device,
                device_id_type=MESH,
            ))
        batch.append(pltpu.make_async_copy(
            x_ref.at[:, pl.ds(pl.multiple_of(me_mode * width + c * chunk, chunk), chunk)], full.at[spot], row_local.at[c]
        ))
        for copy in batch:
            copy.start()
        copies.append(batch)
    pairs = block_pairs(m // LANES)
    in_ref[...] = jnp.zeros_like(in_ref)
    stores = []
    for c in range(CHUNKS):
        for copy in copies[c]:
            copy.wait()
        part = (slice(None), pl.ds(c * chunk, chunk))
        store = pltpu.make_async_copy(full.at[part], full_out.at[part], row_out.at[c])
        store.start()
        stores.append(store)
        x = full[part]
        hi = x.astype(BF16)
        lo = (x - hi.astype(F32)).astype(BF16)
        for i in range(m // LANES):
            top = slice(i * LANES, (i + 1) * LANES)
            strip = nt(hi[top], hi[i * LANES :]) + (nt(hi[top], lo[i * LANES :]) + nt(lo[top], hi[i * LANES :]))
            for j in range(i, m // LANES):
                spot = pl.ds(pairs.index((i, j)) * LANES, LANES)
                in_ref[spot, :] += strip[:, (j - i) * LANES : (j - i + 1) * LANES]
    in_ref[...] = in_ref[...] / total_cols

    def at(start, size):
        return pl.ds(pl.multiple_of(start, SUB), size)

    def exchange(phase, stage, source, target):
        def copy(off):
            other, device = peer(stage, off)
            return pltpu.make_async_remote_copy(
                src_ref=source(other),
                dst_ref=target(mine[stage], off),
                send_sem=send.at[phase, off],
                recv_sem=recv.at[phase, off],
                device_id=device,
                device_id_type=MESH,
            )
        def begin(off, carry):
            copy(off).start()
            return carry
        def end(off, carry):
            copy(off).wait()
            return carry
        lax.fori_loop(1, sizes[stage], begin, 0)
        lax.fori_loop(1, sizes[stage], end, 0)

    def total(stage, source, got):
        def add(off, value):
            return value + got[off - 1]
        return lax.fori_loop(1, sizes[stage], add, source[at(mine[stage] * rows[stage], rows[stage]), :])

    exchange(0, 0, lambda o: in_ref.at[at(o * rows[0], rows[0])], lambda o, off: got1.at[off - 1])
    sum1[...] = total(0, in_ref, got1)
    exchange(1, 1, lambda o: sum1.at[at(o * rows[1], rows[1])], lambda o, off: got2.at[off - 1])
    sum2[...] = total(1, sum1, got2)
    exchange(2, 2, lambda o: sum2.at[at(o * rows[2], rows[2])], lambda o, off: got3.at[off - 1])
    start2 = me_core * rows[0] + me_mode * rows[1]
    start3 = start2 + me_z * rows[2]
    out_ref[at(start3, rows[2]), :] = total(2, sum2, got3)
    for phase, stage, start, size in ((3, 2, start3, rows[2]), (4, 1, start2, rows[1]), (5, 0, me_core * rows[0], rows[0])):
        block = out_ref.at[at(start, size)]
        exchange(phase, stage, lambda o: block, lambda o, off: block)


    for store in stores:
        store.wait()


def gram_sum(unfolded, modes, rest):
    rows_dev, cols_dev = unfolded.shape
    m, width = rows_dev * modes, cols_dev // modes
    cores = 2 if rest % 2 == 0 else 1
    depth = rest // cores
    count = len(block_pairs(m // LANES)) * LANES
    each = pl.cdiv(count, modes * rest * SUB) * SUB
    padded = each * modes * rest
    vmem = pl.BlockSpec(memory_space=pltpu.VMEM)
    anywhere = pl.BlockSpec(memory_space=pl.ANY)
    most = max(cores, modes, depth)
    return pl.pallas_call(
        functools.partial(gram_kernel, (modes, cores, depth), cols_dev * rest),
        out_shape=(jax.ShapeDtypeStruct((m, width), F32), jax.ShapeDtypeStruct((padded, LANES), F32)),
        in_specs=[anywhere],
        out_specs=(anywhere, vmem),
        scratch_shapes=[
            pltpu.VMEM((m, width), F32),
            pltpu.VMEM((padded, LANES), F32),
            pltpu.VMEM((max(cores - 1, 1), padded // cores, LANES), F32),
            pltpu.VMEM((max(modes - 1, 1), padded // (cores * modes), LANES), F32),
            pltpu.VMEM((max(depth - 1, 1), each, LANES), F32),
            pltpu.VMEM((padded // cores, LANES), F32),
            pltpu.VMEM((padded // (cores * modes), LANES), F32),
            pltpu.SemaphoreType.DMA((6, most)),
            pltpu.SemaphoreType.DMA((6, most)),
            pltpu.SemaphoreType.DMA((CHUNKS, modes)),
            pltpu.SemaphoreType.DMA((CHUNKS, modes)),
            pltpu.SemaphoreType.DMA((CHUNKS,)),
            pltpu.SemaphoreType.DMA((CHUNKS,)),
        ],
        compiler_params=pltpu.CompilerParams(
            collective_id=0, has_side_effects=True, vmem_limit_bytes=32 * 1024 * 1024
        ),
        name="gram_sum",
    )(unfolded)


def per_device(unfolded, start_block):
    high = lax.Precision.HIGH
    modes, rest = lax.axis_size("mode"), lax.axis_size("rest")
    full_rows, packed = gram_sum(unfolded, modes, rest)
    triangle, factor, basis_t = solve(packed, start_block)
    partial_value = jnp.dot(basis_t, full_rows, precision=high)
    core = lax.all_to_all(partial_value, "mode", split_axis=0, concat_axis=1, tiled=True)
    return (triangle, factor, core)


def solution(mesh):
    return jax.shard_map(
        per_device,
        mesh=mesh,
        in_specs=(P("mode", "rest"), P()),
        out_specs=(P(), P(), P("mode", "rest")),
        check_vma=False,
    )
```

```python
import functools

import jax
import jax.numpy as jnp
from jax import lax
from jax.experimental import pallas as pl
from jax.experimental.pallas import tpu as pltpu
from jax.sharding import PartitionSpec as P

ITERS = 3
SUB = 8
STEP = 16
CHUNKS = 4
LANES = 128
F32 = jnp.float32
BF16 = jnp.bfloat16
MESH = pl.DeviceIdType.MESH


def parts3(x):
    hi = x.astype(BF16).astype(F32)
    rest = x - hi
    mid = rest.astype(BF16).astype(F32)
    return hi, mid, rest - mid


def nt(x, y):
    return lax.dot_general(x, y, (((1,), (1,)), ((), ())), preferred_element_type=F32)


def nn(x, y):
    return lax.dot_general(x, y, (((1,), (0,)), ((), ())), preferred_element_type=F32)


def dotf(x, y, dims):
    return lax.dot_general(
        x, y, (dims, ((), ())), precision=lax.Precision.HIGHEST, preferred_element_type=F32
    )


def eliminate(ref, row, col, width, block):
    r0 = pl.multiple_of(block * STEP, STEP)
    chunks = [ref[pl.ds(row + r0, STEP), pl.ds(col + c, LANES)] for c in range(0, width, LANES)]
    sub = lax.broadcasted_iota(jnp.int32, (STEP, LANES), 0)
    cols = [
        jnp.take_along_axis(chunks[0], jnp.full((STEP, LANES), r0 + k, jnp.int32), axis=1) for k in range(STEP)
    ]
    pivots = jnp.ones((STEP, LANES), F32)
    for k in range(STEP):
        p = cols[k][k : k + 1, :]
        f = jnp.where(sub > k, cols[k] * (1.0 / p), 0.0)
        pivots = jnp.where(sub == k, p, pivots)
        for j in range(k + 1, STEP):
            cols[j] = cols[j] - f * cols[j][k : k + 1, :]
        chunks = [v - f * v[k : k + 1, :] for v in chunks]
    s = lax.rsqrt(pivots)
    s = s * (1.5 - 0.5 * pivots * s * s)
    chunks = [v * s for v in chunks]
    v = jnp.concatenate(chunks, axis=1)
    ref[pl.ds(row + r0, STEP), pl.ds(col, width)] = v
    lane = lax.broadcasted_iota(jnp.int32, (STEP, LANES), 1)
    keep = lane >= r0 + STEP
    hi, mid, lo = parts3(v)
    lh, lm, ll = (jnp.where(keep, x[:, :LANES], 0.0) for x in (hi, mid, lo))
    left = jnp.concatenate([lh, lh, lm, lm, lh, ll], axis=0).astype(BF16)
    right = jnp.concatenate([hi, mid, hi, mid, lo, hi], axis=0).astype(BF16)
    upd = lax.dot_general(left, right, (((0,), (0,)), ((), ())), preferred_element_type=F32)
    ref[pl.ds(row, LANES), pl.ds(col, width)] -= upd


def block_pairs(count):
    return [(i, j) for i in range(count) for j in range(i, count)]


def solve_kernel(packed_ref, start_ref, work, factor_ref, basis_ref, gram_ref, aug):
    m, r = start_ref.shape
    rounds = m // LANES
    for at, (i, j) in enumerate(block_pairs(rounds)):
        piece = packed_ref[pl.ds(at * LANES, LANES), :]
        spot = (pl.ds(i * LANES, LANES), pl.ds(j * LANES, LANES))
        gram_ref[spot] = piece
        work[spot] = piece
        if i != j:
            gram_ref[spot[::-1]] = piece.T

    def refill(basis_t):
        image_t = dotf(basis_t, gram_ref[...], ((1,), (0,)))
        aug[:, pl.ds(0, r)] = dotf(image_t, image_t, ((1,), (1,)))
        aug[:, pl.ds(r, m)] = image_t

    refill(start_ref[...].T)
    for t in range(max(rounds - 1, ITERS)):
        base = t * LANES

        def step(block, carry):
            if t < rounds - 1:
                eliminate(work, base, base, m - base, block)
            if t < ITERS:
                eliminate(aug, 0, 0, r + m, block)
            return carry

        lax.fori_loop(0, LANES // STEP, step, 0)
        if t < rounds - 1:
            tail = m - base - LANES
            u = work[pl.ds(base, LANES), pl.ds(base + LANES, tail)]
            work[pl.ds(base + LANES, tail), pl.ds(base + LANES, tail)] -= dotf(u, u, ((0,), (0,)))
        if t < ITERS - 1:
            refill(aug[:, pl.ds(r, m)])
    basis_t = aug[:, pl.ds(r, m)]
    basis_ref[...] = basis_t
    factor_ref[...] = basis_t.T


def solve(packed, start_block):
    m, r = start_block.shape
    vmem = pl.BlockSpec(memory_space=pltpu.VMEM)
    return pl.pallas_call(
        solve_kernel,
        out_shape=(
            jax.ShapeDtypeStruct((m, m), F32),
            jax.ShapeDtypeStruct((m, r), F32),
            jax.ShapeDtypeStruct((r, m), F32),
        ),
        in_specs=[vmem, vmem],
        out_specs=(vmem, vmem, vmem),
        scratch_shapes=[pltpu.VMEM((m, m), F32), pltpu.VMEM((r, r + m), F32)],
        compiler_params=pltpu.CompilerParams(vmem_limit_bytes=32 * 1024 * 1024),
        cost_estimate=pl.CostEstimate(
            flops=12 * ITERS * r * m * (m + r) + 4 * m * m * m, bytes_accessed=8 * m * m, transcendentals=m
        ),
        name="solve",
    )(packed, start_block)


def gram_kernel(shape, total_cols, x_ref, full_out, out_ref, full, in_ref, got1, got2, got3, sum1, sum2,
                send, recv, row_send, row_recv, row_local, row_out):
    modes, cores, depth = shape
    me_mode = lax.axis_index("mode")
    me_rest = lax.axis_index("rest")
    me_core = lax.rem(me_rest, cores)
    me_z = me_rest // cores
    mine = (me_core, me_mode, me_z)
    sizes = (cores, modes, depth)
    rows = [in_ref.shape[0] // cores]
    rows.append(rows[0] // modes)
    rows.append(rows[1] // depth)

    def peer(stage, off):
        other = lax.rem(mine[stage] + off, sizes[stage])
        spot = [me_core, me_mode, me_z]
        spot[stage] = other
        return other, (spot[1], spot[2] * cores + spot[0])

    barrier = pltpu.get_barrier_semaphore()
    for stage in range(3):
        def greet(off, carry):
            _, device = peer(stage, off)
            pl.semaphore_signal(barrier, inc=1, device_id=device, device_id_type=MESH)
            return carry
        lax.fori_loop(1, sizes[stage], greet, 0)
    pl.semaphore_wait(barrier, sum(sizes) - 3)

    rows_dev = x_ref.shape[0]
    m, width = full.shape
    chunk = width // CHUNKS
    copies = []
    for c in range(CHUNKS):
        batch = []
        spot = (pl.ds(pl.multiple_of(me_mode * rows_dev, rows_dev), rows_dev), pl.ds(c * chunk, chunk))
        for off in range(1, modes):
            other, device = peer(1, off)
            batch.append(pltpu.make_async_remote_copy(
                src_ref=x_ref.at[:, pl.ds(pl.multiple_of(other * width + c * chunk, chunk), chunk)],
                dst_ref=full.at[spot],
                send_sem=row_send.at[c, off],
                recv_sem=row_recv.at[c, off],
                device_id=device,
                device_id_type=MESH,
            ))
        batch.append(pltpu.make_async_copy(
            x_ref.at[:, pl.ds(pl.multiple_of(me_mode * width + c * chunk, chunk), chunk)], full.at[spot], row_local.at[c]
        ))
        for copy in batch:
            copy.start()
        copies.append(batch)
    pairs = block_pairs(m // LANES)
    in_ref[...] = jnp.zeros_like(in_ref)
    stores = []
    for c in range(CHUNKS):
        for copy in copies[c]:
            copy.wait()
        part = (slice(None), pl.ds(c * chunk, chunk))
        store = pltpu.make_async_copy(full.at[part], full_out.at[part], row_out.at[c])
        store.start()
        stores.append(store)
        x = full[part]
        hi = x.astype(BF16)
        lo = (x - hi.astype(F32)).astype(BF16)
        for i in range(m // LANES):
            top = slice(i * LANES, (i + 1) * LANES)
            strip = nt(hi[top], hi[i * LANES :]) + (nt(hi[top], lo[i * LANES :]) + nt(lo[top], hi[i * LANES :]))
            for j in range(i, m // LANES):
                spot = pl.ds(pairs.index((i, j)) * LANES, LANES)
                in_ref[spot, :] += strip[:, (j - i) * LANES : (j - i + 1) * LANES]
    in_ref[...] = in_ref[...] / total_cols

    def at(start, size):
        return pl.ds(pl.multiple_of(start, SUB), size)

    def exchange(phase, stage, source, target):
        def copy(off):
            other, device = peer(stage, off)
            return pltpu.make_async_remote_copy(
                src_ref=source(other),
                dst_ref=target(mine[stage], off),
                send_sem=send.at[phase, off],
                recv_sem=recv.at[phase, off],
                device_id=device,
                device_id_type=MESH,
            )
        def begin(off, carry):
            copy(off).start()
            return carry
        def end(off, carry):
            copy(off).wait()
            return carry
        lax.fori_loop(1, sizes[stage], begin, 0)
        lax.fori_loop(1, sizes[stage], end, 0)

    def total(stage, source, got):
        def add(off, value):
            return value + got[off - 1]
        return lax.fori_loop(1, sizes[stage], add, source[at(mine[stage] * rows[stage], rows[stage]), :])

    exchange(0, 0, lambda o: in_ref.at[at(o * rows[0], rows[0])], lambda o, off: got1.at[off - 1])
    sum1[...] = total(0, in_ref, got1)
    exchange(1, 1, lambda o: sum1.at[at(o * rows[1], rows[1])], lambda o, off: got2.at[off - 1])
    sum2[...] = total(1, sum1, got2)
    exchange(2, 2, lambda o: sum2.at[at(o * rows[2], rows[2])], lambda o, off: got3.at[off - 1])
    start2 = me_core * rows[0] + me_mode * rows[1]
    start3 = start2 + me_z * rows[2]
    out_ref[at(start3, rows[2]), :] = total(2, sum2, got3)
    for phase, stage, start, size in ((3, 2, start3, rows[2]), (4, 1, start2, rows[1]), (5, 0, me_core * rows[0], rows[0])):
        block = out_ref.at[at(start, size)]
        exchange(phase, stage, lambda o: block, lambda o, off: block)


    for store in stores:
        store.wait()


def gram_sum(unfolded, modes, rest):
    rows_dev, cols_dev = unfolded.shape
    m, width = rows_dev * modes, cols_dev // modes
    cores = 2 if rest % 2 == 0 else 1
    depth = rest // cores
    count = len(block_pairs(m // LANES)) * LANES
    each = pl.cdiv(count, modes * rest * SUB) * SUB
    padded = each * modes * rest
    vmem = pl.BlockSpec(memory_space=pltpu.VMEM)
    anywhere = pl.BlockSpec(memory_space=pltpu.HBM)
    most = max(cores, modes, depth)
    return pl.pallas_call(
        functools.partial(gram_kernel, (modes, cores, depth), cols_dev * rest),
        out_shape=(jax.ShapeDtypeStruct((m, width), F32), jax.ShapeDtypeStruct((padded, LANES), F32)),
        in_specs=[anywhere],
        out_specs=(anywhere, vmem),
        scratch_shapes=[
            pltpu.VMEM((m, width), F32),
            pltpu.VMEM((padded, LANES), F32),
            pltpu.VMEM((max(cores - 1, 1), padded // cores, LANES), F32),
            pltpu.VMEM((max(modes - 1, 1), padded // (cores * modes), LANES), F32),
            pltpu.VMEM((max(depth - 1, 1), each, LANES), F32),
            pltpu.VMEM((padded // cores, LANES), F32),
            pltpu.VMEM((padded // (cores * modes), LANES), F32),
            pltpu.SemaphoreType.DMA((6, most)),
            pltpu.SemaphoreType.DMA((6, most)),
            pltpu.SemaphoreType.DMA((CHUNKS, modes)),
            pltpu.SemaphoreType.DMA((CHUNKS, modes)),
            pltpu.SemaphoreType.DMA((CHUNKS,)),
            pltpu.SemaphoreType.DMA((CHUNKS,)),
        ],
        compiler_params=pltpu.CompilerParams(
            collective_id=0, has_side_effects=True, vmem_limit_bytes=61 * 1024 * 1024
        ),
        name="gram_sum",
    )(unfolded)


def core_kernel(modes, basis_ref, full_ref, work_ref, tri_ref, core_ref, part, last, send, recv):
    me_mode = lax.axis_index("mode")
    me_rest = lax.axis_index("rest")
    rows_dev = core_ref.shape[0]
    width = full_ref.shape[1]
    chunk = width // CHUNKS
    others = [lax.rem(me_mode + off, modes) for off in range(1, modes)]
    barrier = pltpu.get_barrier_semaphore()
    for other in others:
        pl.semaphore_signal(barrier, inc=1, device_id=(other, me_rest), device_id_type=MESH)
    pl.semaphore_wait(barrier, modes - 1)
    basis = basis_ref[...]
    bh = basis.astype(BF16)
    bl = (basis - bh.astype(F32)).astype(BF16)
    copies = []
    for c in range(CHUNKS):
        cols = pl.ds(c * chunk, chunk)
        x = full_ref[:, cols]
        xh = x.astype(BF16)
        xl = (x - xh.astype(F32)).astype(BF16)
        part[:, cols] = nn(bh, xh) + (nn(bh, xl) + nn(bl, xh))
        mine = pl.ds(pl.multiple_of(me_mode * width + c * chunk, chunk), chunk)
        for at, other in enumerate(others):
            copy = pltpu.make_async_remote_copy(
                src_ref=part.at[pl.ds(pl.multiple_of(other * rows_dev, rows_dev), rows_dev), cols],
                dst_ref=core_ref.at[:, mine],
                send_sem=send.at[c, at],
                recv_sem=recv.at[c, at],
                device_id=(other, me_rest),
                device_id_type=MESH,
            )
            copy.start()
            copies.append(copy)
        core_ref[:, mine] = part[pl.ds(pl.multiple_of(me_mode * rows_dev, rows_dev), rows_dev), cols]
    rounds = work_ref.shape[0] // LANES
    base = (rounds - 1) * LANES
    last[...] = work_ref[pl.ds(base, LANES), pl.ds(base, LANES)]

    def step(block, carry):
        eliminate(last, 0, 0, LANES, block)
        return carry

    lax.fori_loop(0, LANES // STEP, step, 0)
    row = lax.broadcasted_iota(jnp.int32, (LANES, LANES), 0)
    col = lax.broadcasted_iota(jnp.int32, (LANES, LANES), 1)
    for i in range(rounds):
        for j in range(rounds):
            spot = (pl.ds(j * LANES, LANES), pl.ds(i * LANES, LANES))
            if j < i:
                tri_ref[spot] = jnp.zeros((LANES, LANES), F32)
                continue
            piece = last[...] if i == rounds - 1 else work_ref[spot[::-1]]
            tri_ref[spot] = (jnp.where(row <= col, piece, 0.0) if i == j else piece).T
    for copy in copies:
        copy.wait()


def core_exchange(basis_t, full_rows, work, modes):
    r = basis_t.shape[0]
    m, width = full_rows.shape
    vmem = pl.BlockSpec(memory_space=pltpu.VMEM)
    return pl.pallas_call(
        functools.partial(core_kernel, modes),
        out_shape=(jax.ShapeDtypeStruct((m, m), F32), jax.ShapeDtypeStruct((r // modes, width * modes), F32)),
        in_specs=[vmem, vmem, vmem],
        out_specs=(vmem, vmem),
        scratch_shapes=[
            pltpu.VMEM((r, width), F32),
            pltpu.VMEM((LANES, LANES), F32),
            pltpu.SemaphoreType.DMA((CHUNKS, modes)),
            pltpu.SemaphoreType.DMA((CHUNKS, modes)),
        ],
        compiler_params=pltpu.CompilerParams(
            collective_id=1, has_side_effects=True, vmem_limit_bytes=32 * 1024 * 1024
        ),
        name="core_exchange",
    )(basis_t, full_rows, work)


def per_device(unfolded, start_block):
    modes, rest = lax.axis_size("mode"), lax.axis_size("rest")
    full_rows, packed = gram_sum(unfolded, modes, rest)
    work, factor, basis_t = solve(packed, start_block)
    triangle, core = core_exchange(basis_t, full_rows, work, modes)
    return (triangle, factor, core)


def solution(mesh):
    return jax.shard_map(
        per_device,
        mesh=mesh,
        in_specs=(P("mode", "rest"), P()),
        out_specs=(P(), P(), P("mode", "rest")),
        check_vma=False,
    )
```

```python
import functools

import jax
import jax.numpy as jnp
from jax import lax
from jax.experimental import pallas as pl
from jax.experimental.pallas import tpu as pltpu
from jax.sharding import PartitionSpec as P

ITERS = 3
SUB = 8
STEP = 16
CHUNKS = 8
LANES = 128
F32 = jnp.float32
BF16 = jnp.bfloat16
MESH = pl.DeviceIdType.MESH


def parts3(x):
    hi = x.astype(BF16).astype(F32)
    rest = x - hi
    mid = rest.astype(BF16).astype(F32)
    return hi, mid, rest - mid


def nt(x, y):
    return lax.dot_general(x, y, (((1,), (1,)), ((), ())), preferred_element_type=F32)


def nn(x, y):
    return lax.dot_general(x, y, (((1,), (0,)), ((), ())), preferred_element_type=F32)


def dotf(x, y, dims):
    return lax.dot_general(
        x, y, (dims, ((), ())), precision=lax.Precision.HIGHEST, preferred_element_type=F32
    )


def eliminate(ref, row, col, width, block):
    r0 = pl.multiple_of(block * STEP, STEP)
    chunks = [ref[pl.ds(row + r0, STEP), pl.ds(col + c, LANES)] for c in range(0, width, LANES)]
    sub = lax.broadcasted_iota(jnp.int32, (STEP, LANES), 0)
    cols = [
        jnp.take_along_axis(chunks[0], jnp.full((STEP, LANES), r0 + k, jnp.int32), axis=1) for k in range(STEP)
    ]
    pivots = jnp.ones((STEP, LANES), F32)
    for k in range(STEP):
        p = cols[k][k : k + 1, :]
        f = jnp.where(sub > k, cols[k] * (1.0 / p), 0.0)
        pivots = jnp.where(sub == k, p, pivots)
        for j in range(k + 1, STEP):
            cols[j] = cols[j] - f * cols[j][k : k + 1, :]
        chunks = [v - f * v[k : k + 1, :] for v in chunks]
    s = lax.rsqrt(pivots)
    s = s * (1.5 - 0.5 * pivots * s * s)
    chunks = [v * s for v in chunks]
    v = jnp.concatenate(chunks, axis=1)
    ref[pl.ds(row + r0, STEP), pl.ds(col, width)] = v
    lane = lax.broadcasted_iota(jnp.int32, (STEP, LANES), 1)
    keep = lane >= r0 + STEP
    hi, mid, lo = parts3(v)
    lh, lm, ll = (jnp.where(keep, x[:, :LANES], 0.0) for x in (hi, mid, lo))
    left = jnp.concatenate([lh, lh, lm, lm, lh, ll], axis=0).astype(BF16)
    right = jnp.concatenate([hi, mid, hi, mid, lo, hi], axis=0).astype(BF16)
    upd = lax.dot_general(left, right, (((0,), (0,)), ((), ())), preferred_element_type=F32)
    ref[pl.ds(row, LANES), pl.ds(col, width)] -= upd


def block_pairs(count):
    return [(i, j) for i in range(count) for j in range(i, count)]


def solve_kernel(packed_ref, start_ref, work, factor_ref, basis_ref, gram_ref, aug):
    m, r = start_ref.shape
    rounds = m // LANES
    for at, (i, j) in enumerate(block_pairs(rounds)):
        piece = packed_ref[pl.ds(at * LANES, LANES), :]
        spot = (pl.ds(i * LANES, LANES), pl.ds(j * LANES, LANES))
        gram_ref[spot] = piece
        work[spot] = piece
        if i != j:
            gram_ref[spot[::-1]] = piece.T

    def refill(basis_t):
        image_t = dotf(basis_t, gram_ref[...], ((1,), (0,)))
        aug[:, pl.ds(0, r)] = dotf(image_t, image_t, ((1,), (1,)))
        aug[:, pl.ds(r, m)] = image_t

    refill(start_ref[...].T)
    for t in range(max(rounds - 1, ITERS)):
        base = t * LANES

        def step(block, carry):
            if t < rounds - 1:
                eliminate(work, base, base, m - base, block)
            if t < ITERS:
                eliminate(aug, 0, 0, r + m, block)
            return carry

        lax.fori_loop(0, LANES // STEP, step, 0)
        if t < rounds - 1:
            tail = m - base - LANES
            u = work[pl.ds(base, LANES), pl.ds(base + LANES, tail)]
            work[pl.ds(base + LANES, tail), pl.ds(base + LANES, tail)] -= dotf(u, u, ((0,), (0,)))
        if t < ITERS - 1:
            refill(aug[:, pl.ds(r, m)])
    basis_t = aug[:, pl.ds(r, m)]
    basis_ref[...] = basis_t
    factor_ref[...] = basis_t.T


def solve(packed, start_block):
    m, r = start_block.shape
    vmem = pl.BlockSpec(memory_space=pltpu.VMEM)
    return pl.pallas_call(
        solve_kernel,
        out_shape=(
            jax.ShapeDtypeStruct((m, m), F32),
            jax.ShapeDtypeStruct((m, r), F32),
            jax.ShapeDtypeStruct((r, m), F32),
        ),
        in_specs=[vmem, vmem],
        out_specs=(vmem, vmem, vmem),
        scratch_shapes=[pltpu.VMEM((m, m), F32), pltpu.VMEM((r, r + m), F32)],
        compiler_params=pltpu.CompilerParams(vmem_limit_bytes=32 * 1024 * 1024),
        cost_estimate=pl.CostEstimate(
            flops=12 * ITERS * r * m * (m + r) + 4 * m * m * m, bytes_accessed=8 * m * m, transcendentals=m
        ),
        name="solve",
    )(packed, start_block)


def gram_kernel(shape, total_cols, x_ref, full_out, out_ref, full, in_ref, got1, got2, got3, sum1, sum2,
                send, recv, row_send, row_recv, row_local, row_out):
    modes, cores, depth = shape
    me_mode = lax.axis_index("mode")
    me_rest = lax.axis_index("rest")
    me_core = lax.rem(me_rest, cores)
    me_z = me_rest // cores
    mine = (me_core, me_mode, me_z)
    sizes = (cores, modes, depth)
    rows = [in_ref.shape[0] // cores]
    rows.append(rows[0] // modes)
    rows.append(rows[1] // depth)

    def peer(stage, off):
        other = lax.rem(mine[stage] + off, sizes[stage])
        spot = [me_core, me_mode, me_z]
        spot[stage] = other
        return other, (spot[1], spot[2] * cores + spot[0])

    barrier = pltpu.get_barrier_semaphore()
    for stage in range(3):
        def greet(off, carry):
            _, device = peer(stage, off)
            pl.semaphore_signal(barrier, inc=1, device_id=device, device_id_type=MESH)
            return carry
        lax.fori_loop(1, sizes[stage], greet, 0)
    pl.semaphore_wait(barrier, sum(sizes) - 3)

    rows_dev = x_ref.shape[0]
    m, width = full.shape
    chunk = width // CHUNKS
    copies = []
    for c in range(CHUNKS):
        batch = []
        spot = (pl.ds(pl.multiple_of(me_mode * rows_dev, rows_dev), rows_dev), pl.ds(c * chunk, chunk))
        for off in range(1, modes):
            other, device = peer(1, off)
            batch.append(pltpu.make_async_remote_copy(
                src_ref=x_ref.at[:, pl.ds(pl.multiple_of(other * width + c * chunk, chunk), chunk)],
                dst_ref=full.at[spot],
                send_sem=row_send.at[c, off],
                recv_sem=row_recv.at[c, off],
                device_id=device,
                device_id_type=MESH,
            ))
        batch.append(pltpu.make_async_copy(
            x_ref.at[:, pl.ds(pl.multiple_of(me_mode * width + c * chunk, chunk), chunk)], full.at[spot], row_local.at[c]
        ))
        for copy in batch:
            copy.start()
        copies.append(batch)
    pairs = block_pairs(m // LANES)
    in_ref[...] = jnp.zeros_like(in_ref)
    stores = []
    for c in range(CHUNKS):
        for copy in copies[c]:
            copy.wait()
        part = (slice(None), pl.ds(c * chunk, chunk))
        store = pltpu.make_async_copy(full.at[part], full_out.at[part], row_out.at[c])
        store.start()
        stores.append(store)
        x = full[part]
        hi = x.astype(BF16)
        lo = (x - hi.astype(F32)).astype(BF16)
        for i in range(m // LANES):
            top = slice(i * LANES, (i + 1) * LANES)
            strip = nt(hi[top], hi[i * LANES :]) + (nt(hi[top], lo[i * LANES :]) + nt(lo[top], hi[i * LANES :]))
            for j in range(i, m // LANES):
                spot = pl.ds(pairs.index((i, j)) * LANES, LANES)
                in_ref[spot, :] += strip[:, (j - i) * LANES : (j - i + 1) * LANES]
    in_ref[...] = in_ref[...] / total_cols

    def at(start, size):
        return pl.ds(pl.multiple_of(start, SUB), size)

    def exchange(phase, stage, source, target):
        def copy(off):
            other, device = peer(stage, off)
            return pltpu.make_async_remote_copy(
                src_ref=source(other),
                dst_ref=target(mine[stage], off),
                send_sem=send.at[phase, off],
                recv_sem=recv.at[phase, off],
                device_id=device,
                device_id_type=MESH,
            )
        def begin(off, carry):
            copy(off).start()
            return carry
        def end(off, carry):
            copy(off).wait()
            return carry
        lax.fori_loop(1, sizes[stage], begin, 0)
        lax.fori_loop(1, sizes[stage], end, 0)

    def total(stage, source, got):
        def add(off, value):
            return value + got[off - 1]
        return lax.fori_loop(1, sizes[stage], add, source[at(mine[stage] * rows[stage], rows[stage]), :])

    exchange(0, 0, lambda o: in_ref.at[at(o * rows[0], rows[0])], lambda o, off: got1.at[off - 1])
    sum1[...] = total(0, in_ref, got1)
    exchange(1, 1, lambda o: sum1.at[at(o * rows[1], rows[1])], lambda o, off: got2.at[off - 1])
    sum2[...] = total(1, sum1, got2)
    exchange(2, 2, lambda o: sum2.at[at(o * rows[2], rows[2])], lambda o, off: got3.at[off - 1])
    start2 = me_core * rows[0] + me_mode * rows[1]
    start3 = start2 + me_z * rows[2]
    out_ref[at(start3, rows[2]), :] = total(2, sum2, got3)
    for phase, stage, start, size in ((3, 2, start3, rows[2]), (4, 1, start2, rows[1]), (5, 0, me_core * rows[0], rows[0])):
        block = out_ref.at[at(start, size)]
        exchange(phase, stage, lambda o: block, lambda o, off: block)


    for store in stores:
        store.wait()


def gram_sum(unfolded, modes, rest):
    rows_dev, cols_dev = unfolded.shape
    m, width = rows_dev * modes, cols_dev // modes
    cores = 2 if rest % 2 == 0 else 1
    depth = rest // cores
    count = len(block_pairs(m // LANES)) * LANES
    each = pl.cdiv(count, modes * rest * SUB) * SUB
    padded = each * modes * rest
    vmem = pl.BlockSpec(memory_space=pltpu.VMEM)
    anywhere = pl.BlockSpec(memory_space=pltpu.HBM)
    most = max(cores, modes, depth)
    return pl.pallas_call(
        functools.partial(gram_kernel, (modes, cores, depth), cols_dev * rest),
        out_shape=(jax.ShapeDtypeStruct((m, width), F32), jax.ShapeDtypeStruct((padded, LANES), F32)),
        in_specs=[anywhere],
        out_specs=(anywhere, vmem),
        scratch_shapes=[
            pltpu.VMEM((m, width), F32),
            pltpu.VMEM((padded, LANES), F32),
            pltpu.VMEM((max(cores - 1, 1), padded // cores, LANES), F32),
            pltpu.VMEM((max(modes - 1, 1), padded // (cores * modes), LANES), F32),
            pltpu.VMEM((max(depth - 1, 1), each, LANES), F32),
            pltpu.VMEM((padded // cores, LANES), F32),
            pltpu.VMEM((padded // (cores * modes), LANES), F32),
            pltpu.SemaphoreType.DMA((6, most)),
            pltpu.SemaphoreType.DMA((6, most)),
            pltpu.SemaphoreType.DMA((CHUNKS, modes)),
            pltpu.SemaphoreType.DMA((CHUNKS, modes)),
            pltpu.SemaphoreType.DMA((CHUNKS,)),
            pltpu.SemaphoreType.DMA((CHUNKS,)),
        ],
        compiler_params=pltpu.CompilerParams(
            collective_id=0, has_side_effects=True, vmem_limit_bytes=61 * 1024 * 1024
        ),
        name="gram_sum",
    )(unfolded)


def core_kernel(modes, basis_ref, full_ref, work_ref, tri_ref, core_ref, part, last, send, recv):
    me_mode = lax.axis_index("mode")
    me_rest = lax.axis_index("rest")
    rows_dev = core_ref.shape[0]
    width = full_ref.shape[1]
    chunk = width // CHUNKS
    others = [lax.rem(me_mode + off, modes) for off in range(1, modes)]
    barrier = pltpu.get_barrier_semaphore()
    for other in others:
        pl.semaphore_signal(barrier, inc=1, device_id=(other, me_rest), device_id_type=MESH)
    pl.semaphore_wait(barrier, modes - 1)
    basis = basis_ref[...]
    bh = basis.astype(BF16)
    bl = (basis - bh.astype(F32)).astype(BF16)
    copies = []
    for c in range(CHUNKS):
        cols = pl.ds(c * chunk, chunk)
        x = full_ref[:, cols]
        xh = x.astype(BF16)
        xl = (x - xh.astype(F32)).astype(BF16)
        part[:, cols] = nn(bh, xh) + (nn(bh, xl) + nn(bl, xh))
        mine = pl.ds(pl.multiple_of(me_mode * width + c * chunk, chunk), chunk)
        for at, other in enumerate(others):
            copy = pltpu.make_async_remote_copy(
                src_ref=part.at[pl.ds(pl.multiple_of(other * rows_dev, rows_dev), rows_dev), cols],
                dst_ref=core_ref.at[:, mine],
                send_sem=send.at[c, at],
                recv_sem=recv.at[c, at],
                device_id=(other, me_rest),
                device_id_type=MESH,
            )
            copy.start()
            copies.append(copy)
        core_ref[:, mine] = part[pl.ds(pl.multiple_of(me_mode * rows_dev, rows_dev), rows_dev), cols]
    rounds = work_ref.shape[0] // LANES
    base = (rounds - 1) * LANES
    last[...] = work_ref[pl.ds(base, LANES), pl.ds(base, LANES)]

    def step(block, carry):
        eliminate(last, 0, 0, LANES, block)
        return carry

    lax.fori_loop(0, LANES // STEP, step, 0)
    row = lax.broadcasted_iota(jnp.int32, (LANES, LANES), 0)
    col = lax.broadcasted_iota(jnp.int32, (LANES, LANES), 1)
    for i in range(rounds):
        for j in range(rounds):
            spot = (pl.ds(j * LANES, LANES), pl.ds(i * LANES, LANES))
            if j < i:
                tri_ref[spot] = jnp.zeros((LANES, LANES), F32)
                continue
            piece = last[...] if i == rounds - 1 else work_ref[spot[::-1]]
            tri_ref[spot] = (jnp.where(row <= col, piece, 0.0) if i == j else piece).T
    for copy in copies:
        copy.wait()


def core_exchange(basis_t, full_rows, work, modes):
    r = basis_t.shape[0]
    m, width = full_rows.shape
    vmem = pl.BlockSpec(memory_space=pltpu.VMEM)
    return pl.pallas_call(
        functools.partial(core_kernel, modes),
        out_shape=(jax.ShapeDtypeStruct((m, m), F32), jax.ShapeDtypeStruct((r // modes, width * modes), F32)),
        in_specs=[vmem, vmem, vmem],
        out_specs=(vmem, vmem),
        scratch_shapes=[
            pltpu.VMEM((r, width), F32),
            pltpu.VMEM((LANES, LANES), F32),
            pltpu.SemaphoreType.DMA((CHUNKS, modes)),
            pltpu.SemaphoreType.DMA((CHUNKS, modes)),
        ],
        compiler_params=pltpu.CompilerParams(
            collective_id=1, has_side_effects=True, vmem_limit_bytes=32 * 1024 * 1024
        ),
        name="core_exchange",
    )(basis_t, full_rows, work)


def per_device(unfolded, start_block):
    modes, rest = lax.axis_size("mode"), lax.axis_size("rest")
    full_rows, packed = gram_sum(unfolded, modes, rest)
    work, factor, basis_t = solve(packed, start_block)
    triangle, core = core_exchange(basis_t, full_rows, work, modes)
    return (triangle, factor, core)


def solution(mesh):
    return jax.shard_map(
        per_device,
        mesh=mesh,
        in_specs=(P("mode", "rest"), P()),
        out_specs=(P(), P(), P("mode", "rest")),
        check_vma=False,
    )
```
